32 devices in a mesh: clip: 2 (over y), row: 16 (over z, x, core).
Axes of the slice: x: 2, y: 2, z: 4, core: 2. Of those that a mesh axis runs over, the one named last changes fastest.
Arguments:
- features: bfloat16 [1, 64, 48, 384], P(None, ('clip', 'row')), parts along dimension 1, may hold values from -19 to 19
- conv_cache: bfloat16 [2, 64, 48, 384], P(None, ('clip', 'row')), parts along dimension 1, may hold values from -6 to 6
- norm_gain: float32 [384], replicated, may hold values from 0.1 to 1.9
- w_query: bfloat16 [384, 384], replicated
- w_key: bfloat16 [384, 384], replicated
- w_value: bfloat16 [384, 384], replicated, may hold values from -0.3125 to 0.3125
- w_out: bfloat16 [384, 384], replicated
- conv_gain: float32 [384], replicated, may hold values from 0.1 to 1.9
- conv_weight: bfloat16 [3, 3, 3, 384, 384], replicated, may hold values from -0.0625 to 0.0625
Outputs:
- residual_out: float32 [1, 64, 48, 384], P(None, ('clip', 'row')), parts along dimension 1
- conv_out: bfloat16 [1, 64, 48, 384], P(None, ('clip', 'row')), parts along dimension 1
The draws below stay inside these ranges and needn't reach their ends.
There are 2 independent parts, one for each index of `clip`. The reference program is written for one: setup_inputs(seed, part) draws one part's arguments, and reference() takes and returns one part's arrays. A program takes and returns all parts, laid end to end along the dimension named above; an argument that names none is the same for every part. Nothing has to cross between parts.
All inputs are finite; a program needn't handle non-finite values.
Results may differ from the reference program's by a relative error of at most 0.0096.
Values may be sent and summed in bfloat16 or wider, within the bound.
A program may use at most 128 MiB of HBM per device.

```python
import math
import jax
import jax.numpy as jnp
from jax import lax

C = 384
F = 1
W = 48
CACHE = 2
H = 32


def base_matrix(key):
    return jnp.clip(jax.random.normal(key, (C, C), jnp.float32), -6.0, 6.0) * C ** (-0.5)


def shared_query(key):
    matrix = base_matrix(jax.random.fold_in(key, 11))
    return matrix * 1.5


def draw_w_query(key, part):
    return shared_query(key).astype(jnp.bfloat16)


def draw_w_key(key, part):
    return (base_matrix(jax.random.fold_in(key, 12)) * 1.5).astype(jnp.bfloat16)


def draw_w_out(key, part):
    values = jnp.clip(jax.random.normal(jax.random.fold_in(key, 22), (C, C), jnp.float32), -6.0, 6.0)
    return (values * 8.0 * C ** (-0.5)).astype(jnp.bfloat16)


def draw_features(key, part):
    first_key = jax.random.fold_in(key, 31)
    noise = jnp.clip(jax.random.normal(first_key, (F, H, W, C), jnp.float32), -6.0, 6.0)
    return noise.astype(jnp.bfloat16)


def block_scale(key, dims, pieces, low, high):
    def one(position, blocks):
        draws = jax.random.uniform(jax.random.fold_in(jax.random.fold_in(key, 6), position), (blocks,), jnp.float32, low / len(pieces), high / len(pieces))
        return jnp.repeat(jnp.exp(draws), dims[position] // blocks).reshape((-1,) + (1,) * (len(dims) - position - 1))

    loudness = one(*pieces[0])
    for cut in pieces[1:]:
        loudness = loudness * one(*cut)
    return loudness


def centred(key, shape, width, bound, shards=(), kind=jnp.bfloat16):
    entries = jax.random.normal(key, shape, jnp.float32) * width
    if len(shards) > 0:
        entries = block_scale(key, shape, shards, -0.22, 0.18) * entries
    return jnp.clip(entries, min=-bound, max=bound).astype(kind)


def setup_inputs(seed: int = 0, part: int = 0) -> dict:
    splits = jax.random.split(jax.random.key(seed), 10)
    part_keys = jax.random.split(jax.random.fold_in(splits[9], part), 10)
    features = draw_features(jax.random.fold_in(jax.random.fold_in(splits[9], part), 71), part)
    conv_cache = centred(part_keys[1], (CACHE, H, W, C), 1.0, 6.0, ((1, 16),))
    norm_gain = jnp.clip(1.0 + 0.18 * jax.random.normal(splits[2], (C,), jnp.float32), 0.1, 1.9)
    w_query = draw_w_query(jax.random.fold_in(splits[9], 71), part)
    w_key = draw_w_key(jax.random.fold_in(splits[9], 71), part)
    w_value = centred(splits[5], (C, C), C ** -0.5, 0.3125)
    w_out = draw_w_out(jax.random.fold_in(splits[9], 71), part)
    conv_gain = jnp.clip(1.0 + 0.18 * jax.random.normal(splits[7], (C,), jnp.float32), 0.1, 1.9)
    conv_weight = centred(splits[8], (3, 3, 3, C, C), (27 * C) ** -0.5, 0.0625)
    return {"features": features, "conv_cache": conv_cache, "norm_gain": norm_gain, "w_query": w_query, "w_key": w_key, "w_value": w_value, "w_out": w_out, "conv_gain": conv_gain, "conv_weight": conv_weight}


def rms_norm(values, gain):
    return values * lax.rsqrt(lax.optimization_barrier(jnp.mean(values * values, axis=-1, keepdims=True)) + 1e-06) * gain

def reference(features, conv_cache, norm_gain, w_query, w_key, w_value, w_out, conv_gain, conv_weight):
    positions = H * W
    source = features.astype(jnp.float32)
    normed = rms_norm(source, norm_gain).astype(jnp.bfloat16).reshape(F * positions, C)

    def project(weight):
        return jnp.dot(normed, weight, preferred_element_type=jnp.float32).astype(jnp.bfloat16).reshape(F, positions, C)
    query = project(w_query)
    keyed = project(w_key)
    valued = project(w_value)
    block = math.gcd(positions, 512)
    score_scale = C ** (-0.5)

    def frame(operands):
        frame_query, frame_keys, frame_values = operands

        def attend(query_block):
            scores = jnp.dot(query_block, frame_keys.T, preferred_element_type=jnp.float32) * score_scale
            expw = jnp.exp(scores - lax.optimization_barrier(jnp.max(scores, axis=-1, keepdims=True)))
            total = lax.optimization_barrier(jnp.sum(expw, axis=-1, keepdims=True))
            summed = jnp.dot(expw.astype(jnp.bfloat16), frame_values, preferred_element_type=jnp.float32)
            return (summed / total).astype(jnp.bfloat16)
        return lax.map(attend, frame_query.reshape(positions // block, block, C)).reshape(positions, C)
    attended = lax.map(frame, (query, keyed, valued))
    residual_out = source + jnp.dot(attended.reshape(F * positions, C), w_out, preferred_element_type=jnp.float32).reshape(F, H, W, C)
    activated = jax.nn.silu(rms_norm(residual_out, conv_gain)).astype(jnp.bfloat16)
    extended = jnp.concatenate([conv_cache, activated], axis=0)
    padded = jnp.pad(extended, ((0, 0), (1, 1), (1, 1), (0, 0)))
    summed = jnp.zeros((F * positions, C), jnp.float32)
    for shift_t in range(3):
        for shift_y in range(3):
            for shift_x in range(3):
                window = padded[shift_t:shift_t + F, shift_y:shift_y + H, shift_x:shift_x + W].reshape(F * positions, C)
                summed = summed + jnp.dot(window, conv_weight[shift_t, shift_y, shift_x], preferred_element_type=jnp.float32)
    conv_out = summed.reshape(F, H, W, C).astype(jnp.bfloat16)
    return (residual_out, conv_out)
```

```python
import functools
import math

import jax
import jax.numpy as jnp
from jax import lax
from jax.experimental import pallas as pl
from jax.experimental.pallas import tpu as pltpu
from jax.sharding import PartitionSpec as P

MESH = pl.DeviceIdType.MESH
F32 = jnp.float32
BF16 = jnp.bfloat16
INNER = 4
UNROLL = 4


def _rms(v, gain):
    return v * lax.rsqrt(jnp.mean(v * v, axis=-1, keepdims=True) + 1e-06) * gain


def _flip(index, bits):
    bit = 1
    while bit <= bits:
        if bits & bit:
            index = index + bit - 2 * bit * ((index // bit) % 2)
        bit *= 2
    return index


def _when(cond):
    if isinstance(cond, bool):
        return (lambda f: f()) if cond else (lambda f: None)
    return pl.when(cond)


def _both(a, b):
    if isinstance(a, bool) and isinstance(b, bool):
        return a and b
    return jnp.logical_and(a, b)


def kernel(
    count,
    width,
    feat_hbm,
    cache_hbm,
    ng_ref,
    wq_hbm,
    wk_hbm,
    wv_hbm,
    wo_hbm,
    cg_ref,
    cw_hbm,
    res_ref,
    out_ref,
    blocks,
    src,
    ext,
    wq,
    wk,
    wv,
    wo,
    cw,
    qs,
    m_ref,
    l_ref,
    acc,
    cacc,
    load_sem,
    cw_sem,
    halo_send,
    halo_recv,
    z_send,
    x_send,
    c_send,
    recv,
):
    outer = count // INNER
    tokens, channels = feat_hbm.shape
    total = tokens + 2 * width
    me = lax.axis_index("row")
    z = me // INNER
    xpeer = me - z * INNER
    pair = (xpeer // 2) % 2
    core = xpeer % 2
    xpeer = me + 2 - 4 * pair
    cpeer = me + 1 - 2 * core
    static = outer <= UNROLL

    def zpeer(step):
        if static:
            return _flip(z, step)
        return lax.rem(z + step, outer)

    def zfrom(step):
        if static:
            return _flip(z, step)
        return lax.rem(z - step + outer, outer)

    def loop(low, high, body):
        if static:
            for step in range(low, high):
                body(step)
        else:
            lax.fori_loop(low, high, lambda i, carry: (body(i), carry)[1], 0)

    has_prev = me > 0
    has_next = me < count - 1
    prev = jnp.maximum(me - 1, 0)
    after = jnp.minimum(me + 1, count - 1)

    own = pl.ds(width, tokens)
    loads = [
        pltpu.make_async_copy(feat_hbm, src.at[own], load_sem.at[0]),
        pltpu.make_async_copy(wq_hbm, wq, load_sem.at[1]),
        pltpu.make_async_copy(wk_hbm, wk, load_sem.at[2]),
        pltpu.make_async_copy(cache_hbm, ext.at[:, own], load_sem.at[3]),
        pltpu.make_async_copy(wv_hbm, wv, load_sem.at[4]),
        pltpu.make_async_copy(wo_hbm, wo, load_sem.at[5]),
    ]
    wloads = [pltpu.make_async_copy(cw_hbm.at[t], cw.at[t], cw_sem.at[t]) for t in range(3)]
    for copy in loads[:4]:
        copy.start()
    for copy in wloads[:2]:
        copy.start()
    for copy in loads[4:]:
        copy.start()
    wloads[2].start()

    barrier = pltpu.get_barrier_semaphore()

    def greet(device):
        pl.semaphore_signal(barrier, inc=1, device_id={"row": device}, device_id_type=MESH)

    def greet_z(step):
        greet(zpeer(step) * INNER + 2 * pair + core)

    loop(1, outer, greet_z)
    greet(xpeer)
    greet(cpeer)

    greet(lax.rem(me + 1, count))
    greet(lax.rem(me + count - 1, count))
    pl.semaphore_wait(barrier, outer + 3)

    def halo(a, b, index, device):
        return pltpu.make_async_remote_copy(
            src_ref=a,
            dst_ref=b,
            send_sem=halo_send.at[index],
            recv_sem=halo_recv.at[index],
            device_id={"row": device},
            device_id_type=MESH,
        )

    first = pl.ds(0, width)
    last = pl.ds(tokens - width, width)
    low = pl.ds(0, width)
    high = pl.ds(width + tokens, width)
    up_f = halo(feat_hbm.at[last], src.at[low], 0, after)
    down_f = halo(feat_hbm.at[first], src.at[high], 1, prev)
    up_c = halo(cache_hbm.at[:, last], ext.at[:, low], 2, after)
    down_c = halo(cache_hbm.at[:, first], ext.at[:, high], 3, prev)

    @pl.when(has_next)
    def _():
        up_f.start()

    @pl.when(has_prev)
    def _():
        down_f.start()

    def put(ident, sem, device):
        return pltpu.make_async_remote_copy(
            src_ref=blocks.at[ident],
            dst_ref=blocks.at[ident],
            send_sem=sem,
            recv_sem=recv.at[ident],
            device_id={"row": device},
            device_id_type=MESH,
        )

    def at(zi, p, c):
        return zi * INNER + 2 * p + c

    def z_put(step):
        return put(me, z_send.at[step], at(zpeer(step), pair, core))

    def x_put(step):
        return put(at(zfrom(step), pair, core), x_send.at[step], xpeer)

    def c_put(step, which):
        p = pair if which == 0 else 1 - pair
        return put(at(zfrom(step), p, core), c_send.at[which, step], cpeer)

    def arrived(ident):
        put(ident, z_send.at[0], cpeer).wait_recv()

    gain = ng_ref[...].reshape(1, channels)
    loads[0].wait()
    blocks[me] = _rms(src[own, :].astype(F32), gain).astype(BF16)
    loop(1, outer, lambda s: z_put(s).start())
    x_put(0).start()
    c_put(0, 0).start()

    @pl.when(has_next)
    def _():
        up_c.start()

    @pl.when(has_prev)
    def _():
        down_c.start()

    zero = jnp.zeros((width, channels), BF16)

    @pl.when(has_prev)
    def _():
        up_f.wait_recv()

    @pl.when(jnp.logical_not(has_prev))
    def _():
        src[low, :] = zero
        for t in range(ext.shape[0]):
            ext[t, low, :] = zero

    @pl.when(has_next)
    def _():
        down_f.wait_recv()

    @pl.when(jnp.logical_not(has_next))
    def _():
        src[high, :] = zero
        for t in range(ext.shape[0]):
            ext[t, high, :] = zero

    loads[1].wait()
    loads[2].wait()
    normed = _rms(src[...].astype(F32), gain).astype(BF16)
    query = jnp.dot(normed, wq[...], preferred_element_type=F32).astype(BF16)
    folded = lax.dot_general(
        query, wk[...], (((1,), (1,)), ((), ())), preferred_element_type=F32
    )
    qs[...] = (folded * (channels**-0.5 * math.log2(math.e))).astype(BF16)
    m_ref[...] = jnp.full(m_ref.shape, -1e30, F32)
    l_ref[...] = jnp.zeros(l_ref.shape, F32)
    acc[...] = jnp.zeros(acc.shape, F32)

    def conv(frame, t):
        taps = jnp.concatenate(
            [frame[dy * width : dy * width + tokens] for dy in range(3)], axis=-1
        )
        for dx in range(3):
            part = jnp.dot(
                taps,
                cw[t, :, dx].reshape(3 * channels, channels),
                preferred_element_type=F32,
            )
            if t == 0:
                cacc[dx] = part
            else:
                cacc[dx] += part

    def attend(step):
        zi = zfrom(step)
        keys = blocks[pl.ds(zi * INNER, INNER)].reshape(INNER * tokens, channels)
        scores = lax.dot_general(
            qs[...], keys, (((1,), (1,)), ((), ())), preferred_element_type=F32
        )
        old = m_ref[...]
        new = jnp.maximum(old, jnp.max(scores, axis=-1, keepdims=True))
        scale = jnp.exp2(old - new)
        expw = jnp.exp2(scores - new)
        m_ref[...] = new
        l_ref[...] = l_ref[...] * scale + jnp.sum(expw, axis=-1, keepdims=True)
        acc[...] = acc[...] * scale + jnp.dot(
            expw.astype(BF16), keys, preferred_element_type=F32
        )

    def stage_z(step):
        arrived(at(zfrom(step), pair, core))
        x_put(step).start()
        c_put(step, 0).start()

    def stage_x(step):
        arrived(at(zfrom(step), 1 - pair, core))
        c_put(step, 1).start()

    def stage_c(step):
        zi = zfrom(step)
        arrived(at(zi, pair, 1 - core))
        arrived(at(zi, 1 - pair, 1 - core))
        attend(step)

    stage_x(0)
    loads[3].wait()

    @pl.when(has_prev)
    def _():
        up_c.wait_recv()

    @pl.when(has_next)
    def _():
        down_c.wait_recv()

    if static:
        for step in range(1, outer + 2):
            if step < outer:
                stage_z(step)
            if 0 < step - 1 < outer:
                stage_x(step - 1)
            if step <= 2:
                wloads[step - 1].wait()
                conv(ext[step - 1], step - 1)
            if 0 <= step - 2 < outer:
                stage_c(step - 2)
    else:
        for t in range(2):
            wloads[t].wait()
            conv(ext[t], t)
        stage_z(1)

        def body(step):
            stage_z(step)
            stage_x(step - 1)
            stage_c(step - 2)

        loop(2, outer, body)
        stage_x(outer - 1)
        stage_c(outer - 2)
        stage_c(outer - 1)

    loads[4].wait()
    loads[5].wait()
    mixed = (acc[...] / l_ref[...]).astype(BF16)
    attended = jnp.dot(mixed, wv[...], preferred_element_type=F32).astype(BF16)
    residual = src[...].astype(F32) + jnp.dot(attended, wo[...], preferred_element_type=F32)
    res_ref[...] = residual[width : width + tokens]
    v = _rms(residual, cg_ref[...].reshape(1, channels))
    activated = v / (1.0 + jnp.exp(-v))
    spot = lax.broadcasted_iota(jnp.int32, (total, 1), 0)
    start = jnp.where(has_prev, 0, width)
    stop = jnp.where(has_next, total, total - width)
    activated = jnp.where((spot >= start) & (spot < stop), activated, 0.0).astype(BF16)
    wloads[2].wait()
    conv(activated, 2)
    column = lax.broadcasted_iota(jnp.int32, (tokens, 1), 0) % width
    left = jnp.where(column == 0, 0.0, pltpu.roll(cacc[0], 1, 0))
    right = jnp.where(column == width - 1, 0.0, pltpu.roll(cacc[2], tokens - 1, 0))
    out_ref[...] = (left + cacc[1] + right).astype(BF16)

    loop(1, outer, lambda s: z_put(s).wait_send())
    loop(0, outer, lambda s: x_put(s).wait_send())
    loop(0, outer, lambda s: c_put(s, 0).wait_send())
    loop(0, outer, lambda s: c_put(s, 1).wait_send())

    @pl.when(has_next)
    def _():
        up_f.wait_send()
        up_c.wait_send()

    @pl.when(has_prev)
    def _():
        down_f.wait_send()
        down_c.wait_send()


def shards(features, conv_cache, norm_gain, w_query, w_key, w_value, w_out, conv_gain, conv_weight):
    frames, rows, width, channels = features.shape
    cached = conv_cache.shape[0]
    tokens = rows * width
    total = tokens + 2 * width
    count = lax.axis_size("row")
    outer = count // INNER
    hbm = pl.BlockSpec(memory_space=pl.ANY)
    vmem = pl.BlockSpec(memory_space=pltpu.VMEM)
    dma = pltpu.SemaphoreType.DMA
    square = pltpu.VMEM((channels, channels), BF16)
    residual, conv_out = pl.pallas_call(
        functools.partial(kernel, count, width),
        out_shape=(
            jax.ShapeDtypeStruct((tokens, channels), F32),
            jax.ShapeDtypeStruct((tokens, channels), BF16),
        ),
        in_specs=[hbm, hbm, vmem, hbm, hbm, hbm, hbm, vmem, hbm],
        out_specs=(vmem, vmem),
        scratch_shapes=[
            pltpu.VMEM((count, tokens, channels), BF16),
            pltpu.VMEM((total, channels), BF16),
            pltpu.VMEM((cached, total, channels), BF16),
            square,
            square,
            square,
            square,
            pltpu.VMEM(conv_weight.shape, BF16),
            pltpu.VMEM((total, channels), BF16),
            pltpu.VMEM((total, 1), F32),
            pltpu.VMEM((total, 1), F32),
            pltpu.VMEM((total, channels), F32),
            pltpu.VMEM((3, tokens, channels), F32),
            dma((6,)),
            dma((3,)),
            dma((4,)),
            dma((4,)),
            dma((outer,)),
            dma((outer,)),
            dma((2, outer)),
            dma((count,)),
        ],
        compiler_params=pltpu.CompilerParams(
            collective_id=0, has_side_effects=True, vmem_limit_bytes=48 << 20
        ),
    )(
        features.reshape(tokens, channels),
        conv_cache.reshape(cached, tokens, channels),
        norm_gain,
        w_query,
        w_key,
        w_value,
        w_out,
        conv_gain,
        conv_weight,
    )
    return (
        residual.reshape(frames, rows, width, channels),
        conv_out.reshape(frames, rows, width, channels),
    )


def solution(mesh):
    placed = (
        P(None, ("clip", "row"), None, None),
        P(None, ("clip", "row"), None, None),
        P(),
        P(),
        P(),
        P(),
        P(),
        P(),
        P(),
    )
    return jax.shard_map(
        shards,
        mesh=mesh,
        in_specs=placed,
        out_specs=(P(None, ("clip", "row"), None, None), P(None, ("clip", "row"), None, None)),
        check_vma=False,
    )
```

```python
import functools
import math

import jax
import jax.numpy as jnp
from jax import lax
from jax.experimental import pallas as pl
from jax.experimental.pallas import tpu as pltpu
from jax.sharding import PartitionSpec as P

MESH = pl.DeviceIdType.MESH
F32 = jnp.float32
BF16 = jnp.bfloat16
INNER = 4
UNROLL = 4


def _rms(v, gain):
    return v * lax.rsqrt(jnp.mean(v * v, axis=-1, keepdims=True) + 1e-06) * gain


def _flip(index, bits):
    bit = 1
    while bit <= bits:
        if bits & bit:
            index = index + bit - 2 * bit * ((index // bit) % 2)
        bit *= 2
    return index


def _when(cond):
    if isinstance(cond, bool):
        return (lambda f: f()) if cond else (lambda f: None)
    return pl.when(cond)


def _both(a, b):
    if isinstance(a, bool) and isinstance(b, bool):
        return a and b
    return jnp.logical_and(a, b)


def kernel(
    count,
    width,
    feat_hbm,
    cache_hbm,
    ng_hbm,
    wq_hbm,
    wk_hbm,
    wv_hbm,
    wo_hbm,
    cg_hbm,
    cw_hbm,
    res_ref,
    out_ref,
    ng_ref,
    cg_ref,
    blocks,
    src,
    ext,
    wq,
    wk,
    wv,
    wo,
    cw,
    qs,
    m_ref,
    l_ref,
    acc,
    cacc,
    load_sem,
    cw_sem,
    halo_send,
    halo_recv,
    z_send,
    x_send,
    c_send,
    recv,
):
    outer = count // INNER
    tokens, channels = feat_hbm.shape
    total = tokens + 2 * width
    me = lax.axis_index("row")
    z = me // INNER
    xpeer = me - z * INNER
    pair = (xpeer // 2) % 2
    core = xpeer % 2
    xpeer = me + 2 - 4 * pair
    cpeer = me + 1 - 2 * core
    static = outer <= UNROLL

    def zpeer(step):
        if static:
            return _flip(z, step)
        return lax.rem(z + step, outer)

    def zfrom(step):
        if static:
            return _flip(z, step)
        return lax.rem(z - step + outer, outer)

    def loop(low, high, body):
        if static:
            for step in range(low, high):
                body(step)
        else:
            lax.fori_loop(low, high, lambda i, carry: (body(i), carry)[1], 0)

    has_prev = me > 0
    has_next = me < count - 1
    prev = jnp.maximum(me - 1, 0)
    after = jnp.minimum(me + 1, count - 1)

    own = pl.ds(width, tokens)
    loads = [
        pltpu.make_async_copy(feat_hbm, src.at[own], load_sem.at[0]),
        pltpu.make_async_copy(wq_hbm, wq, load_sem.at[1]),
        pltpu.make_async_copy(wk_hbm, wk, load_sem.at[2]),
        pltpu.make_async_copy(cache_hbm, ext.at[:, own], load_sem.at[3]),
        pltpu.make_async_copy(wv_hbm, wv, load_sem.at[4]),
        pltpu.make_async_copy(wo_hbm, wo, load_sem.at[5]),
        pltpu.make_async_copy(cg_hbm, cg_ref, load_sem.at[6]),
    ]
    gains = pltpu.make_async_copy(ng_hbm, ng_ref, load_sem.at[7])
    gains.start()
    wloads = [pltpu.make_async_copy(cw_hbm.at[t], cw.at[t], cw_sem.at[t]) for t in range(3)]
    for copy in loads[:4]:
        copy.start()
    for copy in wloads[:2]:
        copy.start()
    for copy in loads[4:]:
        copy.start()
    wloads[2].start()

    barrier = pltpu.get_barrier_semaphore()

    def greet(device):
        pl.semaphore_signal(barrier, inc=1, device_id={"row": device}, device_id_type=MESH)

    def greet_z(step):
        greet(zpeer(step) * INNER + 2 * pair + core)

    loop(1, outer, greet_z)
    greet(xpeer)
    greet(cpeer)

    greet(lax.rem(me + 1, count))
    greet(lax.rem(me + count - 1, count))
    pl.semaphore_wait(barrier, outer + 3)

    def halo(a, b, index, device):
        return pltpu.make_async_remote_copy(
            src_ref=a,
            dst_ref=b,
            send_sem=halo_send.at[index],
            recv_sem=halo_recv.at[index],
            device_id={"row": device},
            device_id_type=MESH,
        )

    first = pl.ds(0, width)
    last = pl.ds(tokens - width, width)
    low = pl.ds(0, width)
    high = pl.ds(width + tokens, width)
    up_f = halo(feat_hbm.at[last], src.at[low], 0, after)
    down_f = halo(feat_hbm.at[first], src.at[high], 1, prev)
    up_c = halo(cache_hbm.at[:, last], ext.at[:, low], 2, after)
    down_c = halo(cache_hbm.at[:, first], ext.at[:, high], 3, prev)

    @pl.when(has_next)
    def _():
        up_f.start()

    @pl.when(has_prev)
    def _():
        down_f.start()

    def put(ident, sem, device):
        return pltpu.make_async_remote_copy(
            src_ref=blocks.at[ident],
            dst_ref=blocks.at[ident],
            send_sem=sem,
            recv_sem=recv.at[ident],
            device_id={"row": device},
            device_id_type=MESH,
        )

    def at(zi, p, c):
        return zi * INNER + 2 * p + c

    def z_put(step):
        return put(me, z_send.at[step], at(zpeer(step), pair, core))

    def x_put(step):
        return put(at(zfrom(step), pair, core), x_send.at[step], xpeer)

    def c_put(step, which):
        p = pair if which == 0 else 1 - pair
        return put(at(zfrom(step), p, core), c_send.at[which, step], cpeer)

    def arrived(ident):
        put(ident, z_send.at[0], cpeer).wait_recv()

    gains.wait()
    gain = ng_ref[...].reshape(1, channels)
    loads[0].wait()
    blocks[me] = _rms(src[own, :].astype(F32), gain).astype(BF16)
    loop(1, outer, lambda s: z_put(s).start())
    x_put(0).start()
    c_put(0, 0).start()

    @pl.when(has_next)
    def _():
        up_c.start()

    @pl.when(has_prev)
    def _():
        down_c.start()

    zero = jnp.zeros((width, channels), BF16)

    @pl.when(has_prev)
    def _():
        up_f.wait_recv()

    @pl.when(jnp.logical_not(has_prev))
    def _():
        src[low, :] = zero
        for t in range(ext.shape[0]):
            ext[t, low, :] = zero

    @pl.when(has_next)
    def _():
        down_f.wait_recv()

    @pl.when(jnp.logical_not(has_next))
    def _():
        src[high, :] = zero
        for t in range(ext.shape[0]):
            ext[t, high, :] = zero

    loads[1].wait()
    loads[2].wait()
    normed = _rms(src[...].astype(F32), gain).astype(BF16)
    query = jnp.dot(normed, wq[...], preferred_element_type=F32).astype(BF16)
    folded = lax.dot_general(
        query, wk[...], (((1,), (1,)), ((), ())), preferred_element_type=F32
    )
    qs[...] = (folded * (channels**-0.5 * math.log2(math.e))).astype(BF16)
    m_ref[...] = jnp.full(m_ref.shape, -1e30, F32)
    l_ref[...] = jnp.zeros(l_ref.shape, F32)
    acc[...] = jnp.zeros(acc.shape, F32)

    def conv(frame, t):
        taps = jnp.concatenate(
            [frame[dy * width : dy * width + tokens] for dy in range(3)], axis=-1
        )
        for dx in range(3):
            part = jnp.dot(
                taps,
                cw[t, :, dx].reshape(3 * channels, channels),
                preferred_element_type=F32,
            )
            if t == 0:
                cacc[dx] = part
            else:
                cacc[dx] += part

    def attend(step):
        zi = zfrom(step)
        keys = blocks[pl.ds(zi * INNER, INNER)].reshape(INNER * tokens, channels)
        scores = lax.dot_general(
            qs[...], keys, (((1,), (1,)), ((), ())), preferred_element_type=F32
        )
        old = m_ref[...]
        new = jnp.maximum(old, jnp.max(scores, axis=-1, keepdims=True))
        scale = jnp.exp2(old - new)
        expw = jnp.exp2(scores - new)
        m_ref[...] = new
        l_ref[...] = l_ref[...] * scale + jnp.sum(expw, axis=-1, keepdims=True)
        acc[...] = acc[...] * scale + jnp.dot(
            expw.astype(BF16), keys, preferred_element_type=F32
        )

    def stage_z(step):
        arrived(at(zfrom(step), pair, core))
        x_put(step).start()
        c_put(step, 0).start()

    def stage_x(step):
        arrived(at(zfrom(step), 1 - pair, core))
        c_put(step, 1).start()

    def stage_c(step):
        zi = zfrom(step)
        arrived(at(zi, pair, 1 - core))
        arrived(at(zi, 1 - pair, 1 - core))
        attend(step)

    stage_x(0)
    loads[3].wait()

    @pl.when(has_prev)
    def _():
        up_c.wait_recv()

    @pl.when(has_next)
    def _():
        down_c.wait_recv()

    if static:
        for step in range(1, outer + 2):
            if step < outer:
                stage_z(step)
            if 0 < step - 1 < outer:
                stage_x(step - 1)
            if step <= 2:
                wloads[step - 1].wait()
                conv(ext[step - 1], step - 1)
            if 0 <= step - 2 < outer:
                stage_c(step - 2)
    else:
        for t in range(2):
            wloads[t].wait()
            conv(ext[t], t)
        stage_z(1)

        def body(step):
            stage_z(step)
            stage_x(step - 1)
            stage_c(step - 2)

        loop(2, outer, body)
        stage_x(outer - 1)
        stage_c(outer - 2)
        stage_c(outer - 1)

    loads[4].wait()
    loads[5].wait()
    loads[6].wait()
    mixed = (acc[...] / l_ref[...]).astype(BF16)
    attended = jnp.dot(mixed, wv[...], preferred_element_type=F32).astype(BF16)
    residual = src[...].astype(F32) + jnp.dot(attended, wo[...], preferred_element_type=F32)
    res_ref[...] = residual[width : width + tokens]
    v = _rms(residual, cg_ref[...].reshape(1, channels))
    activated = v / (1.0 + jnp.exp(-v))
    spot = lax.broadcasted_iota(jnp.int32, (total, 1), 0)
    start = jnp.where(has_prev, 0, width)
    stop = jnp.where(has_next, total, total - width)
    activated = jnp.where((spot >= start) & (spot < stop), activated, 0.0).astype(BF16)
    wloads[2].wait()
    conv(activated, 2)
    column = lax.broadcasted_iota(jnp.int32, (tokens, 1), 0) % width
    left = jnp.where(column == 0, 0.0, pltpu.roll(cacc[0], 1, 0))
    right = jnp.where(column == width - 1, 0.0, pltpu.roll(cacc[2], tokens - 1, 0))
    out_ref[...] = (left + cacc[1] + right).astype(BF16)

    loop(1, outer, lambda s: z_put(s).wait_send())
    loop(0, outer, lambda s: x_put(s).wait_send())
    loop(0, outer, lambda s: c_put(s, 0).wait_send())
    loop(0, outer, lambda s: c_put(s, 1).wait_send())

    @pl.when(has_next)
    def _():
        up_f.wait_send()
        up_c.wait_send()

    @pl.when(has_prev)
    def _():
        down_f.wait_send()
        down_c.wait_send()


def shards(features, conv_cache, norm_gain, w_query, w_key, w_value, w_out, conv_gain, conv_weight):
    frames, rows, width, channels = features.shape
    cached = conv_cache.shape[0]
    tokens = rows * width
    total = tokens + 2 * width
    count = lax.axis_size("row")
    outer = count // INNER
    hbm = pl.BlockSpec(memory_space=pltpu.HBM)
    vmem = pl.BlockSpec(memory_space=pltpu.VMEM)
    dma = pltpu.SemaphoreType.DMA
    square = pltpu.VMEM((channels, channels), BF16)
    residual, conv_out = pl.pallas_call(
        functools.partial(kernel, count, width),
        out_shape=(
            jax.ShapeDtypeStruct((tokens, channels), F32),
            jax.ShapeDtypeStruct((tokens, channels), BF16),
        ),
        in_specs=[hbm] * 9,
        out_specs=(vmem, vmem),
        scratch_shapes=[
            pltpu.VMEM((channels,), F32),
            pltpu.VMEM((channels,), F32),
            pltpu.VMEM((count, tokens, channels), BF16),
            pltpu.VMEM((total, channels), BF16),
            pltpu.VMEM((cached, total, channels), BF16),
            square,
            square,
            square,
            square,
            pltpu.VMEM(conv_weight.shape, BF16),
            pltpu.VMEM((total, channels), BF16),
            pltpu.VMEM((total, 1), F32),
            pltpu.VMEM((total, 1), F32),
            pltpu.VMEM((total, channels), F32),
            pltpu.VMEM((3, tokens, channels), F32),
            dma((8,)),
            dma((3,)),
            dma((4,)),
            dma((4,)),
            dma((outer,)),
            dma((outer,)),
            dma((2, outer)),
            dma((count,)),
        ],
        compiler_params=pltpu.CompilerParams(
            collective_id=0, has_side_effects=True, vmem_limit_bytes=(64 << 20) - 65536
        ),
    )(
        features.reshape(tokens, channels),
        conv_cache.reshape(cached, tokens, channels),
        norm_gain,
        w_query,
        w_key,
        w_value,
        w_out,
        conv_gain,
        conv_weight,
    )
    return (
        residual.reshape(frames, rows, width, channels),
        conv_out.reshape(frames, rows, width, channels),
    )


def solution(mesh):
    placed = (
        P(None, ("clip", "row"), None, None),
        P(None, ("clip", "row"), None, None),
        P(),
        P(),
        P(),
        P(),
        P(),
        P(),
        P(),
    )
    return jax.shard_map(
        shards,
        mesh=mesh,
        in_specs=placed,
        out_specs=(P(None, ("clip", "row"), None, None), P(None, ("clip", "row"), None, None)),
        check_vma=False,
    )
```

```python
import functools
import math

import jax
import jax.numpy as jnp
from jax import lax
from jax.experimental import pallas as pl
from jax.experimental.pallas import tpu as pltpu
from jax.sharding import PartitionSpec as P

MESH = pl.DeviceIdType.MESH
F32 = jnp.float32
BF16 = jnp.bfloat16
INNER = 4
UNROLL = 4


def _rms(v, gain):
    return v * lax.rsqrt(jnp.mean(v * v, axis=-1, keepdims=True) + 1e-06) * gain


def _flip(index, bits):
    bit = 1
    while bit <= bits:
        if bits & bit:
            index = index + bit - 2 * bit * ((index // bit) % 2)
        bit *= 2
    return index


def _when(cond):
    if isinstance(cond, bool):
        return (lambda f: f()) if cond else (lambda f: None)
    return pl.when(cond)


def _both(a, b):
    if isinstance(a, bool) and isinstance(b, bool):
        return a and b
    return jnp.logical_and(a, b)


def kernel(
    count,
    width,
    feat_hbm,
    cache_hbm,
    ng_hbm,
    wq_hbm,
    wk_hbm,
    wv_hbm,
    wo_hbm,
    cg_hbm,
    cw_hbm,
    res_ref,
    out_ref,
    ng_ref,
    cg_ref,
    blocks,
    src,
    ext,
    wq,
    wk,
    wv,
    wo,
    cw,
    qs,
    m_ref,
    l_ref,
    acc,
    cacc,
    load_sem,
    cw_sem,
    halo_send,
    halo_recv,
    z_send,
    x_send,
    c_send,
    recv,
):
    outer = count // INNER
    tokens, channels = feat_hbm.shape
    total = tokens + 2 * width
    me = lax.axis_index("row")
    z = me // INNER
    xpeer = me - z * INNER
    pair = (xpeer // 2) % 2
    core = xpeer % 2
    xpeer = me + 2 - 4 * pair
    cpeer = me + 1 - 2 * core
    static = outer <= UNROLL

    def zpeer(step):
        if static:
            return _flip(z, step)
        return lax.rem(z + step, outer)

    def zfrom(step):
        if static:
            return _flip(z, step)
        return lax.rem(z - step + outer, outer)

    def loop(low, high, body):
        if static:
            for step in range(low, high):
                body(step)
        else:
            lax.fori_loop(low, high, lambda i, carry: (body(i), carry)[1], 0)

    has_prev = me > 0
    has_next = me < count - 1
    prev = jnp.maximum(me - 1, 0)
    after = jnp.minimum(me + 1, count - 1)

    own = pl.ds(width, tokens)
    loads = [
        pltpu.make_async_copy(feat_hbm, src.at[own], load_sem.at[0]),
        pltpu.make_async_copy(wq_hbm, wq, load_sem.at[1]),
        pltpu.make_async_copy(wk_hbm, wk, load_sem.at[2]),
        pltpu.make_async_copy(cache_hbm, ext.at[:, own], load_sem.at[3]),
        pltpu.make_async_copy(wv_hbm, wv, load_sem.at[4]),
        pltpu.make_async_copy(wo_hbm, wo, load_sem.at[5]),
        pltpu.make_async_copy(cg_hbm, cg_ref, load_sem.at[6]),
    ]
    gains = pltpu.make_async_copy(ng_hbm, ng_ref, load_sem.at[7])
    gains.start()
    wloads = [pltpu.make_async_copy(cw_hbm.at[t], cw.at[t], cw_sem.at[t]) for t in range(3)]
    for copy in loads[:4]:
        copy.start()
    for copy in wloads[:2]:
        copy.start()
    for copy in loads[4:]:
        copy.start()
    wloads[2].start()

    barrier = pltpu.get_barrier_semaphore()

    def greet(device):
        pl.semaphore_signal(barrier, inc=1, device_id={"row": device}, device_id_type=MESH)

    def greet_z(step):
        greet(zpeer(step) * INNER + 2 * pair + core)

    loop(1, outer, greet_z)
    greet(xpeer)
    greet(cpeer)

    greet(lax.rem(me + 1, count))
    greet(lax.rem(me + count - 1, count))
    pl.semaphore_wait(barrier, outer + 3)

    def halo(a, b, index, device):
        return pltpu.make_async_remote_copy(
            src_ref=a,
            dst_ref=b,
            send_sem=halo_send.at[index],
            recv_sem=halo_recv.at[index],
            device_id={"row": device},
            device_id_type=MESH,
        )

    first = pl.ds(0, width)
    last = pl.ds(tokens - width, width)
    low = pl.ds(0, width)
    high = pl.ds(width + tokens, width)
    up_f = halo(feat_hbm.at[last], src.at[low], 0, after)
    down_f = halo(feat_hbm.at[first], src.at[high], 1, prev)
    up_c = halo(cache_hbm.at[:, last], ext.at[:, low], 2, after)
    down_c = halo(cache_hbm.at[:, first], ext.at[:, high], 3, prev)

    @pl.when(has_next)
    def _():
        up_f.start()

    @pl.when(has_prev)
    def _():
        down_f.start()

    def put(ident, sem, device):
        return pltpu.make_async_remote_copy(
            src_ref=blocks.at[ident],
            dst_ref=blocks.at[ident],
            send_sem=sem,
            recv_sem=recv.at[ident],
            device_id={"row": device},
            device_id_type=MESH,
        )

    def at(zi, p, c):
        return zi * INNER + 2 * p + c

    def z_put(step):
        return put(me, z_send.at[step], at(zpeer(step), pair, core))

    def x_put(step):
        return put(at(zfrom(step), pair, core), x_send.at[step], xpeer)

    def c_put(step, which):
        p = pair if which == 0 else 1 - pair
        return put(at(zfrom(step), p, core), c_send.at[which, step], cpeer)

    def arrived(ident):
        put(ident, z_send.at[0], cpeer).wait_recv()

    gains.wait()
    gain = ng_ref[...].reshape(1, channels)
    loads[0].wait()
    blocks[me] = _rms(src[own, :].astype(F32), gain).astype(BF16)
    for s in range(1, min(outer, 3)):
        z_put(s).start()
    x_put(0).start()
    c_put(0, 0).start()

    @pl.when(has_next)
    def _():
        up_c.start()

    @pl.when(has_prev)
    def _():
        down_c.start()

    zero = jnp.zeros((width, channels), BF16)

    @pl.when(has_prev)
    def _():
        up_f.wait_recv()

    @pl.when(jnp.logical_not(has_prev))
    def _():
        src[low, :] = zero
        for t in range(ext.shape[0]):
            ext[t, low, :] = zero

    @pl.when(has_next)
    def _():
        down_f.wait_recv()

    @pl.when(jnp.logical_not(has_next))
    def _():
        src[high, :] = zero
        for t in range(ext.shape[0]):
            ext[t, high, :] = zero

    loads[1].wait()
    loads[2].wait()
    normed = _rms(src[...].astype(F32), gain).astype(BF16)
    query = jnp.dot(normed, wq[...], preferred_element_type=F32).astype(BF16)
    folded = lax.dot_general(
        query, wk[...], (((1,), (1,)), ((), ())), preferred_element_type=F32
    )
    qs[...] = (folded * (channels**-0.5 * math.log2(math.e))).astype(BF16)
    m_ref[...] = jnp.full(m_ref.shape, -1e30, F32)
    l_ref[...] = jnp.zeros(l_ref.shape, F32)
    acc[...] = jnp.zeros(acc.shape, F32)

    def conv(frame, t):
        taps = jnp.concatenate(
            [frame[dy * width : dy * width + tokens] for dy in range(3)], axis=-1
        )
        for dx in range(3):
            part = jnp.dot(
                taps,
                cw[t, :, dx].reshape(3 * channels, channels),
                preferred_element_type=F32,
            )
            if t == 0:
                cacc[dx] = part
            else:
                cacc[dx] += part

    def attend(step):
        zi = zfrom(step)
        keys = blocks[pl.ds(zi * INNER, INNER)].reshape(INNER * tokens, channels)
        scores = lax.dot_general(
            qs[...], keys, (((1,), (1,)), ((), ())), preferred_element_type=F32
        )
        old = m_ref[...]
        new = jnp.maximum(old, jnp.max(scores, axis=-1, keepdims=True))
        scale = jnp.exp2(old - new)
        expw = jnp.exp2(scores - new)
        m_ref[...] = new
        l_ref[...] = l_ref[...] * scale + jnp.sum(expw, axis=-1, keepdims=True)
        acc[...] = acc[...] * scale + jnp.dot(
            expw.astype(BF16), keys, preferred_element_type=F32
        )

    def stage_z(step):
        z_put(step).wait_send()

        @_when(step + 2 < outer)
        def _():
            z_put(step + 2).start()

        arrived(at(zfrom(step), pair, core))
        x_put(step).start()
        c_put(step, 0).start()

    def stage_x(step):
        arrived(at(zfrom(step), 1 - pair, core))
        c_put(step, 1).start()

    def stage_c(step):
        zi = zfrom(step)
        arrived(at(zi, pair, 1 - core))
        arrived(at(zi, 1 - pair, 1 - core))
        attend(step)

    stage_x(0)
    loads[3].wait()

    @pl.when(has_prev)
    def _():
        up_c.wait_recv()

    @pl.when(has_next)
    def _():
        down_c.wait_recv()

    if static:
        for step in range(1, outer + 2):
            if step < outer:
                stage_z(step)
            if 0 < step - 1 < outer:
                stage_x(step - 1)
            if step <= 2:
                wloads[step - 1].wait()
                conv(ext[step - 1], step - 1)
            if 0 <= step - 2 < outer:
                stage_c(step - 2)
    else:
        for t in range(2):
            wloads[t].wait()
            conv(ext[t], t)
        stage_z(1)

        def body(step):
            stage_z(step)
            stage_x(step - 1)
            stage_c(step - 2)

        loop(2, outer, body)
        stage_x(outer - 1)
        stage_c(outer - 2)
        stage_c(outer - 1)

    loads[4].wait()
    loads[5].wait()
    loads[6].wait()
    mixed = (acc[...] / l_ref[...]).astype(BF16)
    attended = jnp.dot(mixed, wv[...], preferred_element_type=F32).astype(BF16)
    residual = src[...].astype(F32) + jnp.dot(attended, wo[...], preferred_element_type=F32)
    res_ref[...] = residual[width : width + tokens]
    v = _rms(residual, cg_ref[...].reshape(1, channels))
    activated = v / (1.0 + jnp.exp(-v))
    spot = lax.broadcasted_iota(jnp.int32, (total, 1), 0)
    start = jnp.where(has_prev, 0, width)
    stop = jnp.where(has_next, total, total - width)
    activated = jnp.where((spot >= start) & (spot < stop), activated, 0.0).astype(BF16)
    wloads[2].wait()
    conv(activated, 2)
    column = lax.broadcasted_iota(jnp.int32, (tokens, 1), 0) % width
    left = jnp.where(column == 0, 0.0, pltpu.roll(cacc[0], 1, 0))
    right = jnp.where(column == width - 1, 0.0, pltpu.roll(cacc[2], tokens - 1, 0))
    out_ref[...] = (left + cacc[1] + right).astype(BF16)

    loop(0, outer, lambda s: x_put(s).wait_send())
    loop(0, outer, lambda s: c_put(s, 0).wait_send())
    loop(0, outer, lambda s: c_put(s, 1).wait_send())

    @pl.when(has_next)
    def _():
        up_f.wait_send()
        up_c.wait_send()

    @pl.when(has_prev)
    def _():
        down_f.wait_send()
        down_c.wait_send()


def shards(features, conv_cache, norm_gain, w_query, w_key, w_value, w_out, conv_gain, conv_weight):
    frames, rows, width, channels = features.shape
    cached = conv_cache.shape[0]
    tokens = rows * width
    total = tokens + 2 * width
    count = lax.axis_size("row")
    outer = count // INNER
    hbm = pl.BlockSpec(memory_space=pltpu.HBM)
    vmem = pl.BlockSpec(memory_space=pltpu.VMEM)
    dma = pltpu.SemaphoreType.DMA
    square = pltpu.VMEM((channels, channels), BF16)
    residual, conv_out = pl.pallas_call(
        functools.partial(kernel, count, width),
        out_shape=(
            jax.ShapeDtypeStruct((tokens, channels), F32),
            jax.ShapeDtypeStruct((tokens, channels), BF16),
        ),
        in_specs=[hbm] * 9,
        out_specs=(vmem, vmem),
        scratch_shapes=[
            pltpu.VMEM((channels,), F32),
            pltpu.VMEM((channels,), F32),
            pltpu.VMEM((count, tokens, channels), BF16),
            pltpu.VMEM((total, channels), BF16),
            pltpu.VMEM((cached, total, channels), BF16),
            square,
            square,
            square,
            square,
            pltpu.VMEM(conv_weight.shape, BF16),
            pltpu.VMEM((total, channels), BF16),
            pltpu.VMEM((total, 1), F32),
            pltpu.VMEM((total, 1), F32),
            pltpu.VMEM((total, channels), F32),
            pltpu.VMEM((3, tokens, channels), F32),
            dma((8,)),
            dma((3,)),
            dma((4,)),
            dma((4,)),
            dma((outer,)),
            dma((outer,)),
            dma((2, outer)),
            dma((count,)),
        ],
        compiler_params=pltpu.CompilerParams(
            collective_id=0, has_side_effects=True, vmem_limit_bytes=(64 << 20) - 65536
        ),
    )(
        features.reshape(tokens, channels),
        conv_cache.reshape(cached, tokens, channels),
        norm_gain,
        w_query,
        w_key,
        w_value,
        w_out,
        conv_gain,
        conv_weight,
    )
    return (
        residual.reshape(frames, rows, width, channels),
        conv_out.reshape(frames, rows, width, channels),
    )


def solution(mesh):
    placed = (
        P(None, ("clip", "row"), None, None),
        P(None, ("clip", "row"), None, None),
        P(),
        P(),
        P(),
        P(),
        P(),
        P(),
        P(),
    )
    return jax.shard_map(
        shards,
        mesh=mesh,
        in_specs=placed,
        out_specs=(P(None, ("clip", "row"), None, None), P(None, ("clip", "row"), None, None)),
        check_vma=False,
    )
```

```python
import functools
import math

import jax
import jax.numpy as jnp
from jax import lax
from jax.experimental import pallas as pl
from jax.experimental.pallas import tpu as pltpu
from jax.sharding import PartitionSpec as P

MESH = pl.DeviceIdType.MESH
F32 = jnp.float32
BF16 = jnp.bfloat16
INNER = 4
UNROLL = 4


def _rms(v, gain):
    return v * lax.rsqrt(jnp.mean(v * v, axis=-1, keepdims=True) + 1e-06) * gain


def _flip(index, bits):
    bit = 1
    while bit <= bits:
        if bits & bit:
            index = index + bit - 2 * bit * ((index // bit) % 2)
        bit *= 2
    return index


def _when(cond):
    if isinstance(cond, bool):
        return (lambda f: f()) if cond else (lambda f: None)
    return pl.when(cond)


def _both(a, b):
    if isinstance(a, bool) and isinstance(b, bool):
        return a and b
    return jnp.logical_and(a, b)


def kernel(
    count,
    width,
    feat_hbm,
    cache_hbm,
    ng_hbm,
    wq_hbm,
    wk_hbm,
    wv_hbm,
    wo_hbm,
    cg_hbm,
    cw_hbm,
    res_ref,
    out_ref,
    ng_ref,
    cg_ref,
    blocks,
    src,
    ext,
    wq,
    wk,
    wv,
    wo,
    cw,
    qs,
    m_ref,
    l_ref,
    acc,
    cacc,
    load_sem,
    cw_sem,
    halo_send,
    halo_recv,
    z_send,
    x_send,
    c_send,
    recv,
):
    outer = count // INNER
    tokens, channels = feat_hbm.shape
    total = tokens + 2 * width
    me = lax.axis_index("row")
    z = me // INNER
    xpeer = me - z * INNER
    pair = (xpeer // 2) % 2
    core = xpeer % 2
    xpeer = me + 2 - 4 * pair
    cpeer = me + 1 - 2 * core
    static = outer <= UNROLL

    def zpeer(step):
        if static:
            return _flip(z, step)
        return lax.rem(z + step, outer)

    def zfrom(step):
        if static:
            return _flip(z, step)
        return lax.rem(z - step + outer, outer)

    def loop(low, high, body):
        if static:
            for step in range(low, high):
                body(step)
        else:
            lax.fori_loop(low, high, lambda i, carry: (body(i), carry)[1], 0)

    has_prev = me > 0
    has_next = me < count - 1
    prev = jnp.maximum(me - 1, 0)
    after = jnp.minimum(me + 1, count - 1)

    own = pl.ds(width, tokens)
    loads = [
        pltpu.make_async_copy(feat_hbm, src.at[own], load_sem.at[0]),
        pltpu.make_async_copy(wq_hbm, wq, load_sem.at[1]),
        pltpu.make_async_copy(wk_hbm, wk, load_sem.at[2]),
        pltpu.make_async_copy(cache_hbm, ext.at[:, own], load_sem.at[3]),
        pltpu.make_async_copy(wv_hbm, wv, load_sem.at[4]),
        pltpu.make_async_copy(wo_hbm, wo, load_sem.at[5]),
        pltpu.make_async_copy(cg_hbm, cg_ref, load_sem.at[6]),
    ]
    gains = pltpu.make_async_copy(ng_hbm, ng_ref, load_sem.at[7])
    gains.start()
    wloads = [pltpu.make_async_copy(cw_hbm.at[t], cw.at[t], cw_sem.at[t]) for t in range(3)]
    for copy in loads[:4]:
        copy.start()
    for copy in wloads[:2]:
        copy.start()
    for copy in loads[4:]:
        copy.start()
    wloads[2].start()

    barrier = pltpu.get_barrier_semaphore()

    def greet(device):
        pl.semaphore_signal(barrier, inc=1, device_id={"row": device}, device_id_type=MESH)

    def greet_z(step):
        greet(zpeer(step) * INNER + 2 * pair + core)

    loop(1, outer, greet_z)
    greet(xpeer)
    greet(cpeer)

    greet(lax.rem(me + 1, count))
    greet(lax.rem(me + count - 1, count))
    pl.semaphore_wait(barrier, outer + 3)

    def halo(a, b, index, device):
        return pltpu.make_async_remote_copy(
            src_ref=a,
            dst_ref=b,
            send_sem=halo_send.at[index],
            recv_sem=halo_recv.at[index],
            device_id={"row": device},
            device_id_type=MESH,
        )

    first = pl.ds(0, width)
    last = pl.ds(tokens - width, width)
    low = pl.ds(0, width)
    high = pl.ds(width + tokens, width)
    up_f = halo(feat_hbm.at[last], src.at[low], 0, after)
    down_f = halo(feat_hbm.at[first], src.at[high], 1, prev)
    up_c = halo(cache_hbm.at[:, last], ext.at[:, low], 2, after)
    down_c = halo(cache_hbm.at[:, first], ext.at[:, high], 3, prev)

    @pl.when(has_next)
    def _():
        up_f.start()

    @pl.when(has_prev)
    def _():
        down_f.start()

    def put(ident, sem, device):
        return pltpu.make_async_remote_copy(
            src_ref=blocks.at[ident],
            dst_ref=blocks.at[ident],
            send_sem=sem,
            recv_sem=recv.at[ident],
            device_id={"row": device},
            device_id_type=MESH,
        )

    def at(zi, p, c):
        return zi * INNER + 2 * p + c

    def z_put(step):
        return put(me, z_send.at[step], at(zpeer(step), pair, core))

    def x_put(step):
        return put(at(zfrom(step), pair, core), x_send.at[step], xpeer)

    def c_put(step, which):
        p = pair if which == 0 else 1 - pair
        return put(at(zfrom(step), p, core), c_send.at[which, step], cpeer)

    def arrived(ident):
        put(ident, z_send.at[0], cpeer).wait_recv()

    gains.wait()
    gain = ng_ref[...].reshape(1, channels)
    loads[0].wait()
    blocks[me] = _rms(src[own, :].astype(F32), gain).astype(BF16)
    for s in range(1, min(outer, 3)):
        z_put(s).start()
    x_put(0).start()
    c_put(0, 0).start()

    @pl.when(has_next)
    def _():
        up_c.start()

    @pl.when(has_prev)
    def _():
        down_c.start()

    zero = jnp.zeros((width, channels), BF16)

    @pl.when(has_prev)
    def _():
        up_f.wait_recv()

    @pl.when(jnp.logical_not(has_prev))
    def _():
        src[low, :] = zero
        for t in range(ext.shape[0]):
            ext[t, low, :] = zero

    @pl.when(has_next)
    def _():
        down_f.wait_recv()

    @pl.when(jnp.logical_not(has_next))
    def _():
        src[high, :] = zero
        for t in range(ext.shape[0]):
            ext[t, high, :] = zero

    loads[1].wait()
    loads[2].wait()
    normed = _rms(src[...].astype(F32), gain).astype(BF16)
    query = jnp.dot(normed, wq[...], preferred_element_type=F32).astype(BF16)
    folded = lax.dot_general(
        query, wk[...], (((1,), (1,)), ((), ())), preferred_element_type=F32
    )
    qs[...] = (folded * (channels**-0.5 * math.log2(math.e))).astype(BF16)
    m_ref[...] = jnp.full(m_ref.shape, -1e30, F32)
    l_ref[...] = jnp.zeros(l_ref.shape, F32)
    acc[...] = jnp.zeros(acc.shape, F32)

    def conv(frame, t):
        taps = jnp.concatenate(
            [frame[dy * width : dy * width + tokens] for dy in range(3)], axis=-1
        )
        for dx in range(3):
            part = jnp.dot(
                taps,
                cw[t, :, dx].reshape(3 * channels, channels),
                preferred_element_type=F32,
            )
            if t == 0:
                cacc[dx] = part
            else:
                cacc[dx] += part

    def attend(step):
        zi = zfrom(step)
        keys = blocks[pl.ds(zi * INNER, INNER)].reshape(INNER * tokens, channels)
        scores = lax.dot_general(
            qs[...], keys, (((1,), (1,)), ((), ())), preferred_element_type=F32
        )
        old = m_ref[...]
        new = jnp.maximum(old, jnp.max(scores, axis=-1, keepdims=True))
        scale = jnp.exp2(old - new)
        expw = jnp.exp2(scores - new)
        m_ref[...] = new
        l_ref[...] = l_ref[...] * scale + jnp.sum(expw, axis=-1, keepdims=True)
        acc[...] = acc[...] * scale + jnp.dot(
            expw.astype(BF16), keys, preferred_element_type=F32
        )

    def stage_z(step):
        z_put(step).wait_send()

        @_when(step + 2 < outer)
        def _():
            z_put(step + 2).start()

        arrived(at(zfrom(step), pair, core))
        x_put(step).start()
        c_put(step, 0).start()

    def stage_x(step):
        arrived(at(zfrom(step), 1 - pair, core))
        c_put(step, 1).start()

    def stage_c(step):
        zi = zfrom(step)
        arrived(at(zi, pair, 1 - core))
        arrived(at(zi, 1 - pair, 1 - core))
        attend(step)

    stage_x(0)
    loads[3].wait()

    @pl.when(has_prev)
    def _():
        up_c.wait_recv()

    @pl.when(has_next)
    def _():
        down_c.wait_recv()

    if static:
        for step in range(1, outer + 2):
            if step < outer:
                stage_z(step)
            if 0 < step - 1 < outer:
                stage_x(step - 1)
            if step <= 2:
                wloads[step - 1].wait()
                conv(ext[step - 1], step - 1)
            if 0 <= step - 2 < outer:
                stage_c(step - 2)
    else:
        for t in range(2):
            wloads[t].wait()
            conv(ext[t], t)
        stage_z(1)

        def body(step):
            stage_z(step)
            stage_x(step - 1)
            stage_c(step - 2)

        loop(2, outer, body)
        stage_x(outer - 1)
        stage_c(outer - 2)
        stage_c(outer - 1)

    loads[4].wait()
    loads[5].wait()
    loads[6].wait()
    mixed = (acc[...] / l_ref[...]).astype(BF16)
    attended = jnp.dot(mixed, wv[...], preferred_element_type=F32).astype(BF16)
    residual = src[...].astype(F32) + jnp.dot(attended, wo[...], preferred_element_type=F32)
    res_ref[...] = residual[width : width + tokens]
    v = _rms(residual, cg_ref[...].reshape(1, channels))
    activated = v / (1.0 + jnp.exp(-v))
    spot = lax.broadcasted_iota(jnp.int32, (total, 1), 0)
    start = jnp.where(has_prev, 0, width)
    stop = jnp.where(has_next, total, total - width)
    activated = jnp.where((spot >= start) & (spot < stop), activated, 0.0).astype(BF16)
    wloads[2].wait()
    conv(activated, 2)
    column = lax.broadcasted_iota(jnp.int32, (tokens, 1), 0) % width
    left = jnp.where(column == 0, 0.0, pltpu.roll(cacc[0], 1, 0))
    right = jnp.where(column == width - 1, 0.0, pltpu.roll(cacc[2], tokens - 1, 0))
    out_ref[...] = (left + cacc[1] + right).astype(BF16)

    loop(0, outer, lambda s: x_put(s).wait_send())
    loop(0, outer, lambda s: c_put(s, 0).wait_send())
    loop(0, outer, lambda s: c_put(s, 1).wait_send())

    @pl.when(has_next)
    def _():
        up_f.wait_send()
        up_c.wait_send()

    @pl.when(has_prev)
    def _():
        down_f.wait_send()
        down_c.wait_send()


def shards(features, conv_cache, norm_gain, w_query, w_key, w_value, w_out, conv_gain, conv_weight):
    frames, rows, width, channels = features.shape
    cached = conv_cache.shape[0]
    tokens = rows * width
    total = tokens + 2 * width
    count = lax.axis_size("row")
    outer = count // INNER
    hbm = pl.BlockSpec(memory_space=pltpu.HBM)
    vmem = pl.BlockSpec(memory_space=pltpu.VMEM)
    dma = pltpu.SemaphoreType.DMA
    square = pltpu.VMEM((channels, channels), BF16)
    residual, conv_out = pl.pallas_call(
        functools.partial(kernel, count, width),
        out_shape=(
            jax.ShapeDtypeStruct((tokens, channels), F32),
            jax.ShapeDtypeStruct((tokens, channels), BF16),
        ),
        in_specs=[hbm] * 9,
        out_specs=(vmem, vmem),
        scratch_shapes=[
            pltpu.VMEM((channels,), F32),
            pltpu.VMEM((channels,), F32),
            pltpu.VMEM((count, tokens, channels), BF16),
            pltpu.VMEM((total, channels), BF16),
            pltpu.VMEM((cached, total, channels), BF16),
            square,
            square,
            square,
            square,
            pltpu.VMEM(conv_weight.shape, BF16),
            pltpu.VMEM((total, channels), BF16),
            pltpu.VMEM((total, 1), F32),
            pltpu.VMEM((total, 1), F32),
            pltpu.VMEM((total, channels), F32),
            pltpu.VMEM((3, tokens, channels), F32),
            dma((8,)),
            dma((3,)),
            dma((4,)),
            dma((4,)),
            dma((outer,)),
            dma((outer,)),
            dma((2, outer)),
            dma((count,)),
        ],
        compiler_params=pltpu.CompilerParams(
            collective_id=0, has_side_effects=True, vmem_limit_bytes=48 << 20
        ),
    )(
        *(
            pltpu.with_memory_space_constraint(x, pltpu.HBM)
            for x in (
                features.reshape(tokens, channels),
                conv_cache.reshape(cached, tokens, channels),
                norm_gain,
                w_query,
                w_key,
                w_value,
                w_out,
                conv_gain,
                conv_weight,
            )
        )
    )
    return (
        residual.reshape(frames, rows, width, channels),
        conv_out.reshape(frames, rows, width, channels),
    )


def solution(mesh):
    placed = (
        P(None, ("clip", "row"), None, None),
        P(None, ("clip", "row"), None, None),
        P(),
        P(),
        P(),
        P(),
        P(),
        P(),
        P(),
    )
    return jax.shard_map(
        shards,
        mesh=mesh,
        in_specs=placed,
        out_specs=(P(None, ("clip", "row"), None, None), P(None, ("clip", "row"), None, None)),
        check_vma=False,
    )
```

```python
import functools
import math

import jax
import jax.numpy as jnp
from jax import lax
from jax.experimental import pallas as pl
from jax.experimental.pallas import tpu as pltpu
from jax.sharding import PartitionSpec as P

MESH = pl.DeviceIdType.MESH
F32 = jnp.float32
BF16 = jnp.bfloat16
INNER = 4
UNROLL = 4
HALVES = 1
ORDER = (3, 1, 2)


def _rms(v, gain):
    return v * lax.rsqrt(jnp.mean(v * v, axis=-1, keepdims=True) + 1e-06) * gain


def _flip(index, bits):
    bit = 1
    while bit <= bits:
        if bits & bit:
            index = index + bit - 2 * bit * ((index // bit) % 2)
        bit *= 2
    return index


def _when(cond):
    if isinstance(cond, bool):
        return (lambda f: f()) if cond else (lambda f: None)
    return pl.when(cond)


def _both(a, b):
    if isinstance(a, bool) and isinstance(b, bool):
        return a and b
    return jnp.logical_and(a, b)


def kernel(
    count,
    width,
    feat_hbm,
    cache_hbm,
    ng_hbm,
    wq_hbm,
    wk_hbm,
    wv_hbm,
    wo_hbm,
    cg_hbm,
    cw_hbm,
    res_ref,
    out_ref,
    ng_ref,
    cg_ref,
    blocks,
    src,
    ext,
    wq,
    wk,
    wv,
    wo,
    cw,
    qs,
    m_ref,
    l_ref,
    acc,
    cacc,
    load_sem,
    cw_sem,
    halo_send,
    halo_recv,
    z_send,
    x_send,
    c_send,
    recv,
):
    outer = count // INNER
    tokens, channels = feat_hbm.shape
    total = tokens + 2 * width
    me = lax.axis_index("row")
    z = me // INNER
    xpeer = me - z * INNER
    pair = (xpeer // 2) % 2
    core = xpeer % 2
    xpeer = me + 2 - 4 * pair
    cpeer = me + 1 - 2 * core
    static = outer == UNROLL
    piece = tokens // HALVES

    def zpeer(step):
        if static:
            return _flip(z, step)
        return lax.rem(z + step, outer)

    def zfrom(step):
        if static:
            return _flip(z, step)
        return lax.rem(z - step + outer, outer)

    def loop(low, high, body):
        if static:
            for step in range(low, high):
                body(step)
        else:
            lax.fori_loop(low, high, lambda i, carry: (body(i), carry)[1], 0)

    has_prev = me > 0
    has_next = me < count - 1
    prev = jnp.maximum(me - 1, 0)
    after = jnp.minimum(me + 1, count - 1)

    own = pl.ds(width, tokens)
    loads = [
        pltpu.make_async_copy(feat_hbm, src.at[own], load_sem.at[0]),
        pltpu.make_async_copy(wq_hbm, wq, load_sem.at[1]),
        pltpu.make_async_copy(wk_hbm, wk, load_sem.at[2]),
        pltpu.make_async_copy(cache_hbm, ext.at[:, own], load_sem.at[3]),
        pltpu.make_async_copy(wv_hbm, wv, load_sem.at[4]),
        pltpu.make_async_copy(wo_hbm, wo, load_sem.at[5]),
        pltpu.make_async_copy(cg_hbm, cg_ref, load_sem.at[6]),
    ]
    gains = pltpu.make_async_copy(ng_hbm, ng_ref, load_sem.at[7])
    gains.start()
    wloads = [pltpu.make_async_copy(cw_hbm.at[t], cw.at[t], cw_sem.at[t]) for t in range(3)]
    for copy in loads[:4]:
        copy.start()
    for copy in wloads[:2]:
        copy.start()
    for copy in loads[4:]:
        copy.start()
    wloads[2].start()

    barrier = pltpu.get_barrier_semaphore()

    def greet(device):
        pl.semaphore_signal(barrier, inc=1, device_id={"row": device}, device_id_type=MESH)

    def greet_z(step):
        greet(zpeer(step) * INNER + 2 * pair + core)

    loop(1, outer, greet_z)
    greet(xpeer)
    greet(cpeer)

    greet(lax.rem(me + 1, count))
    greet(lax.rem(me + count - 1, count))
    pl.semaphore_wait(barrier, outer + 3)

    def halo(a, b, index, device):
        return pltpu.make_async_remote_copy(
            src_ref=a,
            dst_ref=b,
            send_sem=halo_send.at[index],
            recv_sem=halo_recv.at[index],
            device_id={"row": device},
            device_id_type=MESH,
        )

    first = pl.ds(0, width)
    last = pl.ds(tokens - width, width)
    low = pl.ds(0, width)
    high = pl.ds(width + tokens, width)
    up_f = halo(feat_hbm.at[last], src.at[low], 0, after)
    down_f = halo(feat_hbm.at[first], src.at[high], 1, prev)
    up_c = halo(cache_hbm.at[:, last], ext.at[:, low], 2, after)
    down_c = halo(cache_hbm.at[:, first], ext.at[:, high], 3, prev)

    @pl.when(has_next)
    def _():
        up_f.start()

    @pl.when(has_prev)
    def _():
        down_f.start()

    def put(ident, h, sem, device):
        part = blocks.at[ident, pl.ds(h * piece, piece)]
        return pltpu.make_async_remote_copy(
            src_ref=part,
            dst_ref=part,
            send_sem=sem,
            recv_sem=recv.at[ident, h],
            device_id={"row": device},
            device_id_type=MESH,
        )

    def at(zi, p, c):
        return zi * INNER + 2 * p + c

    def z_put(step, h):
        if static and step == 2:
            return put(at(zpeer(3), pair, core), h, z_send.at[2, h], at(zpeer(1), pair, core))
        return put(me, h, z_send.at[step, h], at(zpeer(step), pair, core))

    def x_put(step, h):
        return put(at(zfrom(step), pair, core), h, x_send.at[step, h], xpeer)

    def c_put(step, h, which):
        p = pair if which == 0 else 1 - pair
        return put(at(zfrom(step), p, core), h, c_send.at[which, step, h], cpeer)

    def arrived(ident, h):
        put(ident, h, z_send.at[0, h], cpeer).wait_recv()

    gains.wait()
    gain = ng_ref[...].reshape(1, channels)
    loads[0].wait()
    blocks[me] = _rms(src[own, :].astype(F32), gain).astype(BF16)
    opening = [s for s in ORDER if s != 2] if static else range(1, min(outer, 3))
    for s in opening:
        for h in range(HALVES):
            if s == opening[0] or not static:
                z_put(s, h).start()
            if s == opening[0]:
                x_put(0, h).start()
    for h in range(HALVES):
        c_put(0, h, 0).start()

    @pl.when(has_next)
    def _():
        up_c.start()

    @pl.when(has_prev)
    def _():
        down_c.start()

    zero = jnp.zeros((width, channels), BF16)

    @pl.when(has_prev)
    def _():
        up_f.wait_recv()

    @pl.when(jnp.logical_not(has_prev))
    def _():
        src[low, :] = zero
        for t in range(ext.shape[0]):
            ext[t, low, :] = zero

    @pl.when(has_next)
    def _():
        down_f.wait_recv()

    @pl.when(jnp.logical_not(has_next))
    def _():
        src[high, :] = zero
        for t in range(ext.shape[0]):
            ext[t, high, :] = zero

    if static:
        z_put(opening[0], 0).wait_send()
        z_put(opening[1], 0).start()
    loads[1].wait()
    loads[2].wait()
    normed = _rms(src[...].astype(F32), gain).astype(BF16)
    query = jnp.dot(normed, wq[...], preferred_element_type=F32).astype(BF16)
    folded = lax.dot_general(
        query, wk[...], (((1,), (1,)), ((), ())), preferred_element_type=F32
    )
    qs[...] = (folded * (channels**-0.5 * math.log2(math.e))).astype(BF16)
    m_ref[...] = jnp.full(m_ref.shape, -1e30, F32)
    l_ref[...] = jnp.zeros(l_ref.shape, F32)
    acc[...] = jnp.zeros(acc.shape, F32)

    def conv(frame, t):
        taps = jnp.concatenate(
            [frame[dy * width : dy * width + tokens] for dy in range(3)], axis=-1
        )
        for dx in range(3):
            part = jnp.dot(
                taps,
                cw[t, :, dx].reshape(3 * channels, channels),
                preferred_element_type=F32,
            )
            if t == 0:
                cacc[dx] = part
            else:
                cacc[dx] += part

    def attend(step):
        zi = zfrom(step)
        keys = blocks[pl.ds(zi * INNER, INNER)].reshape(INNER * tokens, channels)
        scores = lax.dot_general(
            qs[...], keys, (((1,), (1,)), ((), ())), preferred_element_type=F32
        )
        old = m_ref[...]
        new = jnp.maximum(old, jnp.max(scores, axis=-1, keepdims=True))
        scale = jnp.exp2(old - new)
        expw = jnp.exp2(scores - new)
        m_ref[...] = new
        l_ref[...] = l_ref[...] * scale + jnp.sum(expw, axis=-1, keepdims=True)
        acc[...] = acc[...] * scale + jnp.dot(
            expw.astype(BF16), keys, preferred_element_type=F32
        )

    def stage_z(step, h):
        if not static:
            z_put(step, h).wait_send()

            @pl.when(step + 2 < outer)
            def _():
                z_put(step + 2, h).start()

        arrived(at(zfrom(step), pair, core), h)
        if static and step == 3:
            z_put(2, h).start()
        x_put(step, h).start()
        c_put(step, h, 0).start()

    def stage_x(step, h):
        arrived(at(zfrom(step), 1 - pair, core), h)
        c_put(step, h, 1).start()

    def stage_c(step, h):
        zi = zfrom(step)
        arrived(at(zi, pair, 1 - core), h)
        arrived(at(zi, 1 - pair, 1 - core), h)
        if h == HALVES - 1:
            attend(step)

    loads[3].wait()

    @pl.when(has_prev)
    def _():
        up_c.wait_recv()

    @pl.when(has_next)
    def _():
        down_c.wait_recv()

    if static:
        zunits = [(s, h) for s in ORDER for h in range(HALVES)]
        units = [(0, h) for h in range(HALVES)] + zunits
        for i in range(len(units) + 1):
            if i < len(zunits):
                stage_z(*zunits[i])
            if i < len(units):
                stage_x(*units[i])
            if i < 2:
                wloads[i].wait()
                conv(ext[i], i)
            if i > 0:
                stage_c(*units[i - 1])
    else:
        pieces = range(HALVES)
        for t in range(2):
            wloads[t].wait()
            conv(ext[t], t)
        for h in pieces:
            stage_x(0, h)
        for h in pieces:
            stage_z(1, h)

        def body(step):
            for h in pieces:
                stage_z(step, h)
            for h in pieces:
                stage_x(step - 1, h)
            for h in pieces:
                stage_c(step - 2, h)

        loop(2, outer, body)
        for h in pieces:
            stage_x(outer - 1, h)
        for s in (outer - 2, outer - 1):
            for h in pieces:
                stage_c(s, h)

    loads[4].wait()
    loads[5].wait()
    loads[6].wait()
    mixed = (acc[...] / l_ref[...]).astype(BF16)
    attended = jnp.dot(mixed, wv[...], preferred_element_type=F32).astype(BF16)
    residual = src[...].astype(F32) + jnp.dot(attended, wo[...], preferred_element_type=F32)
    res_ref[...] = residual[width : width + tokens]
    v = _rms(residual, cg_ref[...].reshape(1, channels))
    activated = v / (1.0 + jnp.exp(-v))
    spot = lax.broadcasted_iota(jnp.int32, (total, 1), 0)
    start = jnp.where(has_prev, 0, width)
    stop = jnp.where(has_next, total, total - width)
    activated = jnp.where((spot >= start) & (spot < stop), activated, 0.0).astype(BF16)
    wloads[2].wait()
    conv(activated, 2)
    column = lax.broadcasted_iota(jnp.int32, (tokens, 1), 0) % width
    left = jnp.where(column == 0, 0.0, pltpu.roll(cacc[0], 1, 0))
    right = jnp.where(column == width - 1, 0.0, pltpu.roll(cacc[2], tokens - 1, 0))
    out_ref[...] = (left + cacc[1] + right).astype(BF16)

    for h in range(HALVES):
        if static:
            for s in (opening[1], 2):
                z_put(s, h).wait_send()
        loop(0, outer, lambda s: x_put(s, h).wait_send())
        loop(0, outer, lambda s: c_put(s, h, 0).wait_send())
        loop(0, outer, lambda s: c_put(s, h, 1).wait_send())

    @pl.when(has_next)
    def _():
        up_f.wait_send()
        up_c.wait_send()

    @pl.when(has_prev)
    def _():
        down_f.wait_send()
        down_c.wait_send()


def shards(features, conv_cache, norm_gain, w_query, w_key, w_value, w_out, conv_gain, conv_weight):
    frames, rows, width, channels = features.shape
    cached = conv_cache.shape[0]
    tokens = rows * width
    total = tokens + 2 * width
    count = lax.axis_size("row")
    outer = count // INNER
    hbm = pl.BlockSpec(memory_space=pltpu.HBM)
    vmem = pl.BlockSpec(memory_space=pltpu.VMEM)
    dma = pltpu.SemaphoreType.DMA
    square = pltpu.VMEM((channels, channels), BF16)
    residual, conv_out = pl.pallas_call(
        functools.partial(kernel, count, width),
        out_shape=(
            jax.ShapeDtypeStruct((tokens, channels), F32),
            jax.ShapeDtypeStruct((tokens, channels), BF16),
        ),
        in_specs=[hbm] * 9,
        out_specs=(vmem, vmem),
        scratch_shapes=[
            pltpu.VMEM((channels,), F32),
            pltpu.VMEM((channels,), F32),
            pltpu.VMEM((count, tokens, channels), BF16),
            pltpu.VMEM((total, channels), BF16),
            pltpu.VMEM((cached, total, channels), BF16),
            square,
            square,
            square,
            square,
            pltpu.VMEM(conv_weight.shape, BF16),
            pltpu.VMEM((total, channels), BF16),
            pltpu.VMEM((total, 1), F32),
            pltpu.VMEM((total, 1), F32),
            pltpu.VMEM((total, channels), F32),
            pltpu.VMEM((3, tokens, channels), F32),
            dma((8,)),
            dma((3,)),
            dma((4,)),
            dma((4,)),
            dma((outer, HALVES)),
            dma((outer, HALVES)),
            dma((2, outer, HALVES)),
            dma((count, HALVES)),
        ],
        compiler_params=pltpu.CompilerParams(
            collective_id=0, has_side_effects=True, vmem_limit_bytes=48 << 20
        ),
    )(
        *(
            pltpu.with_memory_space_constraint(x, pltpu.HBM)
            for x in (
                features.reshape(tokens, channels),
                conv_cache.reshape(cached, tokens, channels),
                norm_gain,
                w_query,
                w_key,
                w_value,
                w_out,
                conv_gain,
                conv_weight,
            )
        )
    )
    return (
        residual.reshape(frames, rows, width, channels),
        conv_out.reshape(frames, rows, width, channels),
    )


def solution(mesh):
    placed = (
        P(None, ("clip", "row"), None, None),
        P(None, ("clip", "row"), None, None),
        P(),
        P(),
        P(),
        P(),
        P(),
        P(),
        P(),
    )
    return jax.shard_map(
        shards,
        mesh=mesh,
        in_specs=placed,
        out_specs=(P(None, ("clip", "row"), None, None), P(None, ("clip", "row"), None, None)),
        check_vma=False,
    )
```
